128 devices in a mesh: layer: 8 (over z_hi, x), feat: 16 (over z_lo, y, core).
Axes of the slice: x: 4, y: 4, z: 4 (z_hi: 2, z_lo: 2; z = z_hi * 2 + z_lo), core: 2. Of those that a mesh axis runs over, the one named last changes fastest.
Arguments:
- activations: bfloat16 [4, 1024, 32768], P(None, None, ('layer', 'feat')), may hold values from -6 to 6
- active_blocks: int32 [4, 1024, 256], P(None, None, ('layer', 'feat')), may hold values from 0 to 1, as said below
- cotangent: bfloat16 [4, 1024, 2048], P(None, 'layer', 'feat'), may hold values from -6 to 6
- decoder: bfloat16 [10, 32768, 2048], P(None, ('layer', 'feat')), may hold values from -0.03125 to 0.03125
Outputs:
- decoder_grad: bfloat16 [10, 32768, 2048], P(None, ('layer', 'feat'))
- feature_grad: bfloat16 [4, 1024, 32768], P(None, None, ('layer', 'feat'))
The draws below stay inside these ranges and needn't reach their ends.
Inputs may be any that keep to these rules, and one draw needn't show every extreme that they name: `active_blocks`: 1 where the block of 128 features is active for that token at that layer, else 0.
All inputs are finite; a program needn't handle non-finite values.
Results may differ from the reference program's by a relative error of at most 0.001.
Values may be sent and summed in bfloat16 or wider, within the bound.
A program may use at most 128 MiB of HBM per device.

```python
import jax
import jax.numpy as jnp

D = 2048
BLOCK = 128
LAYERS = 4
TOKENS = 1024
PAIRS = 10
F = 32768


def draw_active_blocks(key, part):
    first_key, second_key = jax.random.split(jax.random.fold_in(key, 17))
    levels = jax.random.randint(first_key, (1, 1, F // BLOCK), 1, 6)
    raw_bits = jax.random.randint(second_key, (LAYERS, TOKENS, F // BLOCK), 0, 6)
    return (raw_bits < levels).astype(jnp.int32)


def shard_levels(own_key, shape, shards, low, largest):
    loudness = 1.0
    for axis_at, parts in shards:
        draws = jax.random.uniform(jax.random.fold_in(jax.random.fold_in(own_key, 6), axis_at), (parts,), jnp.float32, low / len(shards), largest / len(shards))
        loudness = loudness * jnp.repeat(jnp.exp(draws), shape[axis_at] // parts).reshape((-1,) + (1,) * (len(shape) - 1 - axis_at))
    return loudness


def noise(key, shape, scale, bound, pieces=(), kind=jnp.bfloat16):
    factor_of = shard_levels(key, shape, pieces, -0.22, 0.18) if pieces else 1.0
    array = jax.random.normal(key, shape, jnp.float32) * scale * factor_of
    return jnp.minimum(jnp.maximum(array, -bound), bound).astype(kind)


def setup_inputs(seed: int = 0) -> dict:
    keys = jax.random.split(jax.random.key(seed), 5)
    return {
        "activations": noise(keys[0], (LAYERS, TOKENS, F), 1.0, 6.0, ((2, 128),)),
        "active_blocks": draw_active_blocks(jax.random.fold_in(keys[4], 71), 0),
        "cotangent": noise(keys[2], (LAYERS, TOKENS, D), 1.0, 6.0, ((1, 8), (2, 16))),
        "decoder": noise(keys[3], (PAIRS, F, D), F ** -0.5, 0.03125, ((1, 128),)),
    }


def reference(activations, active_blocks, cotangent, decoder):
    feature_mask = jnp.repeat(active_blocks, BLOCK, axis=2).astype(jnp.float32)
    sparse = (activations.astype(jnp.float32) * feature_mask).astype(jnp.bfloat16)
    partial_value = jnp.zeros((LAYERS, TOKENS, F), jnp.float32)
    grads = []
    index = 0
    for target in range(LAYERS):
        upstream = cotangent[target]
        for source in range(target + 1):
            grads.append(jnp.dot(sparse[source].T, upstream, preferred_element_type=jnp.float32).astype(jnp.bfloat16))
            term = jnp.dot(upstream, decoder[index].T, preferred_element_type=jnp.float32)
            partial_value = partial_value.at[source].add(term)
            index = index + 1
    return jnp.stack(grads), (partial_value * feature_mask).astype(jnp.bfloat16)
```

```python
import functools

import jax
import jax.numpy as jnp
from jax import lax
from jax.experimental import pallas as pl
from jax.experimental.pallas import tpu as pltpu
from jax.sharding import PartitionSpec as P

MESH = pl.DeviceIdType.MESH
LAYERS, TOKENS, D, WIDTH = 4, 1024, 2048, 256
PAIRS = LAYERS * (LAYERS + 1) // 2
ROWS = {3: (48, 48, 32), 2: (48, 32, 48), 1: (32, 48, 48), 0: (48, 48, 32)}
START = {g: (0, r[0], r[0] + r[1]) for g, r in ROWS.items()}
ORDER = ((0, 1, 2), (1, 2, 0), (2, 0, 1))
TARGETS = (3, 2, 1, 0)
OFFSET = (0, 1, 3, 6)
BUFS = [(g, a) for g in range(LAYERS) for a in range(3)]
BF16, F32 = jnp.bfloat16, jnp.float32


def position():
    layer, feat = lax.axis_index("layer"), lax.axis_index("feat")
    x, zh = lax.rem(layer, 4), layer // 4
    core, y, zl = lax.rem(feat, 2), lax.rem(feat // 2, 4), feat // 8
    return (x, y, zh * 2 + zl), core


def device_id(c, core):
    x, y, z = c
    return ((z // 2) * 4 + x, (lax.rem(z, 2) * 4 + y) * 2 + core)


def shifted(c, axis, by):
    return tuple(lax.rem(v + by + 4, 4) if i == axis else v for i, v in enumerate(c))


class Gather:
    def __init__(self, own_ref, bufs, own_sem, send, recv):
        self.c, self.core = position()
        self.own_ref, self.bufs = own_ref, dict(zip(BUFS, bufs))
        self.own_sem, self.send, self.recv = own_sem, send, recv
        self.sends, self.copies = [], {}

    def near(self, axis, by):
        return device_id(shifted(self.c, axis, by), self.core)

    def barrier(self):
        sem = pltpu.get_barrier_semaphore()
        peers = [self.near(axis, by) for axis in range(3) for by in (1, -1)]
        peers.append(device_id(self.c, 1 - self.core))
        for peer in peers:
            pl.semaphore_signal(sem, inc=1, device_id=peer, device_id_type=MESH)
        pl.semaphore_wait(sem, len(peers))

    def own(self):
        out = []
        for i, (g, a) in enumerate(BUFS):
            c1, c2, c3 = (self.c[k] for k in ORDER[a])
            out.append(pltpu.make_async_copy(
                self.own_ref.at[g, pl.ds(START[g][a], ROWS[g][a])],
                self.bufs[g, a].at[self.core, c3, c2, c1], self.own_sem.at[i]))
        return out

    def view(self, g, a, key, c):
        c1, c2, c3 = (c[k] for k in ORDER[a])
        buf = self.bufs[g, a].at[self.core]
        if key[0] == "1":
            return buf.at[c3, c2, c1]
        if key[0] == "2":
            return buf.at[c3, c2]
        if key[0] == "3":
            return buf.at[c3, pl.ds(2 * int(key[1]), 2)]
        return buf.at[c3]

    SLOTS = ("1L", "1R", "1O", "2L", "2R", "2O", "30L", "31L", "30R", "31R", "30O", "31O",
             "p0", "pL", "pR", "pO")

    def copy(self, g, a, slot, src, to):
        i = (g * 3 + a) * len(self.SLOTS) + self.SLOTS.index(slot)
        return pltpu.make_async_remote_copy(
            src_ref=src, dst_ref=src, send_sem=self.send.at[i], recv_sem=self.recv.at[i],
            device_id=to, device_id_type=MESH)

    def start(self, g, a, slot, key, by):
        phase = slot[0]
        if phase == "p":
            src = self.view(g, a, "p", shifted(self.c, ORDER[a][2], by))
            to = device_id(self.c, 1 - self.core)
        else:
            axis = ORDER[a][int(phase) - 1]
            src = self.view(g, a, key, shifted(self.c, axis, by))
            if slot[-1] == "O":
                step = -by
            else:
                step = 1 if slot[-1] == "L" else -1
            to = self.near(axis, step)
        copy = self.copy(g, a, slot, src, to)
        copy.start()
        self.copies[g, a, slot] = copy

    def wait(self, g, a, slot):
        self.copies[g, a, slot].wait_recv()

    def p1_start(self, g):
        for a in range(3):
            self.start(g, a, "1L", "1", 0)
            self.start(g, a, "1R", "1", 0)

    def p1_forward(self, g):
        for a in range(3):
            self.wait(g, a, "1L")
            self.wait(g, a, "1R")
            self.start(g, a, "1O", "1", -1 if (g + a) % 2 else 1)

    def p2_start(self, g):
        for a in range(3):
            self.wait(g, a, "1O")
            self.start(g, a, "2L", "2", 0)
            self.start(g, a, "2R", "2", 0)

    def p2_forward(self, g):
        for a in range(3):
            self.wait(g, a, "2L")
            self.wait(g, a, "2R")
            self.start(g, a, "2O", "2", -1 if (g + a) % 2 else 1)

    def p3_start(self, g):
        for a in range(3):
            self.wait(g, a, "2O")
            self.start(g, a, "30L", "30", 0)
            self.start(g, a, "31R", "31", 0)
            self.start(g, a, "31L", "31", 0)
            self.start(g, a, "30R", "30", 0)
            self.start(g, a, "p0", "p", 0)

    def p3_forward(self, g):
        for a in range(3):
            self.wait(g, a, "30L")
            self.start(g, a, "30O", "30", -1)
            self.wait(g, a, "31R")
            self.start(g, a, "31O", "31", 1)

    def partner_sides(self, g):
        for a in range(3):
            self.wait(g, a, "31L")
            self.start(g, a, "pL", "p", -1)
            self.wait(g, a, "30R")
            self.start(g, a, "pR", "p", 1)

    def partner_last(self, g):
        for a in range(3):
            self.wait(g, a, "30O")
            self.wait(g, a, "31O")
            self.start(g, a, "pO", "p", 2)

    def arrived(self, g):
        for a in range(3):
            for slot in ("p0", "pL", "pR", "pO"):
                self.wait(g, a, slot)

    def finish(self):
        for copy in self.copies.values():
            copy.wait_send()


def gather_kernel(own_ref, *rest):
    bufs, (own_sem, send, recv) = rest[:12], rest[12:]
    net = Gather(own_ref, bufs, own_sem, send, recv)
    own = net.own()
    for copy in own:
        copy.start()
    net.barrier()
    for copy in own:
        copy.wait()
    for g in TARGETS:
        net.p1_start(g)
    for g in TARGETS:
        net.p1_forward(g)
    net.p2_start(3)
    net.p2_start(2)
    net.p2_forward(3)
    net.p2_forward(2)
    net.p3_start(3)
    net.p2_start(1)
    net.p3_forward(3)
    net.p2_forward(1)
    net.p3_start(2)
    net.p2_start(0)
    net.partner_sides(3)
    net.p3_forward(2)
    net.partner_last(3)
    net.p2_forward(0)
    net.p3_start(1)
    net.partner_sides(2)
    net.p3_forward(1)
    net.partner_last(2)
    net.arrived(3)
    net.p3_start(0)
    net.partner_sides(1)
    net.p3_forward(0)
    net.partner_last(1)
    net.arrived(2)
    net.partner_sides(0)
    net.partner_last(0)
    net.arrived(1)
    net.arrived(0)
    net.finish()


def gather(cotangent):
    sems = len(BUFS) * len(Gather.SLOTS)
    return pl.pallas_call(
        gather_kernel,
        out_shape=[pltpu.VMEM((2, 4, 4, 4, ROWS[g][a], 128), BF16) for g, a in BUFS],
        in_specs=[pl.BlockSpec(memory_space=pl.ANY)],
        out_specs=[pl.BlockSpec(memory_space=pltpu.VMEM)] * len(BUFS),
        scratch_shapes=[
            pltpu.SemaphoreType.DMA((len(BUFS),)),
            pltpu.SemaphoreType.DMA((sems,)),
            pltpu.SemaphoreType.DMA((sems,)),
        ],
        compiler_params=pltpu.CompilerParams(collective_id=0, has_side_effects=True, vmem_limit_bytes=2 * 2**20),
        name="torus_gather",
    )(cotangent)


def block(bufs, g, x, y, z, core):
    parts = []
    for a in range(3):
        c1, c2, c3 = ((x, y, z)[k] for k in ORDER[a])
        parts.append(bufs[g, a][core, c3, c2, c1])
    return jnp.concatenate(parts, axis=0)


def columns(bufs, g, q):
    zl, y = q // 4, lax.rem(q, 4)
    return jnp.concatenate(
        [jnp.concatenate([block(bufs, g, l % 4, y, (l // 4) * 2 + zl, core) for l in range(8)], axis=0)
         for core in range(2)], axis=1)


def rows(bufs, g, h):
    zh = h // 2
    out = []
    for i in range(2):
        x = lax.rem(h, 2) * 2 + i
        out.append(jnp.concatenate(
            [block(bufs, g, x, (f // 2) % 4, zh * 2 + f // 8, f % 2) for f in range(16)], axis=1))
    return jnp.concatenate(out, axis=0)


def prepare(act, mask, sparse_t, mask_cols):
    for s in range(LAYERS):
        @pl.loop(0, 8)
        def _(l):
            tok = pl.ds(pl.multiple_of(l * 128, 128), 128)
            for b in range(2):
                m = jnp.broadcast_to(mask[s, b:b + 1, tok].astype(F32), (128, 128))
                values = act[s, tok, b * 128:(b + 1) * 128].astype(F32).T
                sparse_t[s, b * 128:(b + 1) * 128, tok] = (values * m).astype(BF16)
                mask_cols[s, tok, b * 128:(b + 1) * 128] = m.T.astype(BF16)


def grad_step(bufs, g, q, sparse_t, store):
    lhs = sparse_t[0:g + 1].reshape((g + 1) * WIDTH, TOKENS)
    out = jnp.dot(lhs, columns(bufs, g, q), preferred_element_type=F32).astype(BF16)
    store(q, out.reshape(g + 1, WIDTH, 256))


def feature_step(bufs, g, h, dec, total, first):
    tok = pl.ds(pl.multiple_of(h * 256, 256), 256)
    lhs = rows(bufs, g, h)
    for s in range(g + 1):
        term = lax.dot_general(lhs, dec[s], (((1,), (1,)), ((), ())), preferred_element_type=F32)
        if first:
            total[s, tok] = term
        else:
            total[s, tok] += term


def compute_kernel(act_hbm, mask, dec_hbm, *rest):
    bufs = dict(zip(BUFS, rest[:12]))
    grad_hbm, feat_hbm, act, sparse_t, mask_cols, dec, total, grad, feat, sem = rest[12:]
    loads = [pltpu.make_async_copy(act_hbm, act, sem.at[0])]
    for g in TARGETS:
        loads.append(pltpu.make_async_copy(dec_hbm.at[pl.ds(OFFSET[g], g + 1)], dec.at[pl.ds(OFFSET[g], g + 1)], sem.at[1 + g]))
    for load in loads:
        load.start()
    loads[0].wait()
    prepare(act, mask, sparse_t, mask_cols)
    stores = []
    for i, g in enumerate(TARGETS):
        base = OFFSET[g]
        def store(q, out):
            grad[base:base + g + 1, :, pl.ds(pl.multiple_of(q * 256, 256), 256)] = out
        @pl.loop(0, 8)
        def _(q):
            grad_step(bufs, g, q, sparse_t, store)
        out = pltpu.make_async_copy(grad.at[pl.ds(base, g + 1)], grad_hbm.at[pl.ds(base, g + 1)], sem.at[5 + g])
        out.start()
        stores.append(out)
        loads[1 + i].wait()
        @pl.loop(0, 4)
        def _(h):
            feature_step(bufs, g, h, dec.at[pl.ds(base, g + 1)], total, i == 0)
    for s in range(LAYERS):
        @pl.loop(0, 8)
        def _(l):
            tok = pl.ds(pl.multiple_of(l * 128, 128), 128)
            feat[s, tok] = (total[s, tok] * mask_cols[s, tok].astype(F32)).astype(BF16)
        out = pltpu.make_async_copy(feat.at[s], feat_hbm.at[s], sem.at[9 + s])
        out.start()
        stores.append(out)
    for out in stores:
        out.wait()


def compute(act, mask, dec, bufs):
    vmem = pl.BlockSpec(memory_space=pltpu.VMEM)
    hbm = pl.BlockSpec(memory_space=pl.ANY)
    return pl.pallas_call(
        compute_kernel,
        out_shape=[jax.ShapeDtypeStruct((PAIRS, WIDTH, D), BF16), jax.ShapeDtypeStruct((LAYERS, TOKENS, WIDTH), BF16)],
        in_specs=[hbm, vmem, hbm] + [vmem] * len(BUFS),
        out_specs=[hbm, hbm],
        scratch_shapes=[
            pltpu.VMEM((LAYERS, TOKENS, WIDTH), BF16),
            pltpu.VMEM((LAYERS, WIDTH, TOKENS), BF16),
            pltpu.VMEM((LAYERS, TOKENS, WIDTH), BF16),
            pltpu.VMEM((PAIRS, WIDTH, D), BF16),
            pltpu.VMEM((LAYERS, TOKENS, WIDTH), F32),
            pltpu.VMEM((PAIRS, WIDTH, D), BF16),
            pltpu.VMEM((LAYERS, TOKENS, WIDTH), BF16),
            pltpu.SemaphoreType.DMA((16,)),
        ],
        compiler_params=pltpu.CompilerParams(vmem_limit_bytes=44 * 2**20),
        name="pair_products",
    )(act, mask, dec, *bufs)


def body(activations, active_blocks, cotangent, decoder):
    bufs = gather(cotangent)
    mask = jnp.transpose(active_blocks, (0, 2, 1))
    return tuple(compute(activations, mask, decoder, bufs))


def solution(mesh):
    in_specs = (
        P(None, None, ("layer", "feat")),
        P(None, None, ("layer", "feat")),
        P(None, "layer", "feat"),
        P(None, ("layer", "feat"), None),
    )
    out_specs = (P(None, ("layer", "feat"), None), P(None, None, ("layer", "feat")))
    return jax.shard_map(body, mesh=mesh, in_specs=in_specs, out_specs=out_specs, check_vma=False)
```

```python
import functools

import jax
import jax.numpy as jnp
from jax import lax
from jax.experimental import pallas as pl
from jax.experimental.pallas import tpu as pltpu
from jax.sharding import PartitionSpec as P

MESH = pl.DeviceIdType.MESH
LAYERS, TOKENS, D, WIDTH = 4, 1024, 2048, 256
PAIRS = LAYERS * (LAYERS + 1) // 2
ROWS = {3: (48, 48, 32), 2: (48, 32, 48), 1: (32, 48, 48), 0: (48, 48, 32)}
START = {g: (0, r[0], r[0] + r[1]) for g, r in ROWS.items()}
ORDER = ((0, 1, 2), (1, 2, 0), (2, 0, 1))
TARGETS = (3, 2, 1, 0)
OFFSET = (0, 1, 3, 6)
BUFS = [(g, a) for g in range(LAYERS) for a in range(3)]
BF16, F32 = jnp.bfloat16, jnp.float32
DIRECT = (3,)
EARLY_LIMIT, LATE_LIMIT = 32 * 2**20, 6 * 2**20


def position():
    layer, feat = lax.axis_index("layer"), lax.axis_index("feat")
    x, zh = lax.rem(layer, 4), layer // 4
    core, y, zl = lax.rem(feat, 2), lax.rem(feat // 2, 4), feat // 8
    return (x, y, zh * 2 + zl), core


def device_id(c, core):
    x, y, z = c
    return ((z // 2) * 4 + x, (lax.rem(z, 2) * 4 + y) * 2 + core)


def shifted(c, axis, by):
    return tuple(lax.rem(v + by + 4, 4) if i == axis else v for i, v in enumerate(c))


class Gather:
    SLOTS = ("1L", "1R", "1O", "2L", "2R", "2O", "3L0", "3L1", "3R0", "3R1", "3O0", "3O1", "p0", "pL", "pR", "pO")

    def __init__(self, own_ref, bufs, own_sem, send, recv):
        self.c, self.core = position()
        self.own_ref, self.bufs = own_ref, bufs
        self.own_sem, self.send, self.recv = own_sem, send, recv

    def near(self, axis, by):
        return device_id(shifted(self.c, axis, by), self.core)

    def greet(self):
        sem = pltpu.get_barrier_semaphore()
        for peer in self.peers():
            pl.semaphore_signal(sem, inc=1, device_id=peer, device_id_type=MESH)

    def peers(self):
        out = [self.near(axis, by) for axis in range(3) for by in (1, -1, 2)]
        return out + [device_id(self.c, 1 - self.core)]

    def meet(self):
        pl.semaphore_wait(pltpu.get_barrier_semaphore(), 10)

    def own(self):
        out = []
        for i, (g, a) in enumerate(BUFS):
            c1, c2, c3 = (self.c[k] for k in ORDER[a])
            out.append(pltpu.make_async_copy(
                self.own_ref.at[g, pl.ds(START[g][a], ROWS[g][a])],
                self.bufs[g, a].at[self.core, c3, c2, c1], self.own_sem.at[i]))
        return out

    def copy(self, g, a, slot):
        phase, side = slot[0], slot[1]
        axis = ORDER[a][2 if phase == "p" else int(phase) - 1]
        by = 0
        if phase == "p":
            by = {"0": 0, "L": -1, "R": 1, "O": 2}[side]
            to = device_id(self.c, 1 - self.core)
        elif side == "O":
            if phase == "1" or (phase == "2" and g in DIRECT):
                to = self.near(axis, 2)
            else:
                by = (-1 if slot[2] == "0" else 1) if phase == "3" else (-1 if (g + a) % 2 else 1)
                to = self.near(axis, -by)
        else:
            to = self.near(axis, 1 if side == "L" else -1)
        c1, c2, c3 = (shifted(self.c, axis, by)[k] for k in ORDER[a])
        buf = self.bufs[g, a].at[self.core, c3]
        if phase == "1":
            buf = buf.at[c2, c1]
        elif phase == "2":
            buf = buf.at[c2]
        elif phase == "3":
            buf = buf.at[pl.ds(2 * int(slot[2]), 2)]
        i = (g * 3 + a) * len(self.SLOTS) + self.SLOTS.index(slot)
        return pltpu.make_async_remote_copy(
            src_ref=buf, dst_ref=buf, send_sem=self.send.at[i], recv_sem=self.recv.at[i],
            device_id=to, device_id_type=MESH)

    def go(self, g, a, *slots):
        for slot in slots:
            self.copy(g, a, slot).start()

    def wait(self, g, a, *slots):
        for slot in slots:
            self.copy(g, a, slot).wait_recv()

    def p1(self, g):
        for a in range(3):
            self.go(g, a, "1O", "1L", "1R")

    def p2(self, g):
        for a in range(3):
            self.wait(g, a, "1O", "1L", "1R")
            if g in DIRECT:
                self.go(g, a, "2O")
            self.go(g, a, "2L", "2R")

    def p2_forward(self, g):
        for a in range(3):
            self.wait(g, a, "2L", "2R")
            self.go(g, a, "2O")

    def p3(self, g):
        for a in range(3):
            if g in DIRECT:
                self.wait(g, a, "2L", "2R")
            self.wait(g, a, "2O")
            self.go(g, a, "3L0", "3R1", "3L1", "3R0")
        for a in range(3):
            self.go(g, a, "p0")

    def p3_forward(self, g):
        for a in range(3):
            self.wait(g, a, "3L0")
            self.go(g, a, "3O0")
            self.wait(g, a, "3R1")
            self.go(g, a, "3O1")

    def sides(self, g):
        for a in range(3):
            self.wait(g, a, "3L1")
            self.go(g, a, "pL")
            self.wait(g, a, "3R0")
            self.go(g, a, "pR")

    def last(self, g):
        for a in range(3):
            self.wait(g, a, "3O0", "3O1")
            self.go(g, a, "pO")

    def arrived(self, g):
        for a in range(3):
            self.wait(g, a, "p0", "pL", "pR", "pO")

    def finish(self):
        for g, a in BUFS:
            for slot in self.SLOTS:
                self.copy(g, a, slot).wait_send()


def block(bufs, g, x, y, z, core):
    parts = []
    for a in range(3):
        c1, c2, c3 = ((x, y, z)[k] for k in ORDER[a])
        parts.append(bufs[g, a][core, c3, c2, c1])
    return jnp.concatenate(parts, axis=0)


def columns(bufs, g, q):
    zl, y = q // 4, lax.rem(q, 4)
    return jnp.concatenate(
        [jnp.concatenate([block(bufs, g, l % 4, y, (l // 4) * 2 + zl, core) for l in range(8)], axis=0)
         for core in range(2)], axis=1)


def rows(bufs, g, h):
    zh = h // 2
    out = []
    for i in range(2):
        x = lax.rem(h, 2) * 2 + i
        out.append(jnp.concatenate(
            [block(bufs, g, x, (f // 2) % 4, zh * 2 + f // 8, f % 2) for f in range(16)], axis=1))
    return jnp.concatenate(out, axis=0)


def prepare(s, act, mask, sparse_t, mask_cols):
    @pl.loop(0, 8)
    def _(l):
        tok = pl.ds(pl.multiple_of(l * 128, 128), 128)
        for b in range(2):
            m = jnp.broadcast_to(mask[s, b:b + 1, tok].astype(F32), (128, 128))
            values = act[s, tok, b * 128:(b + 1) * 128].astype(F32).T
            sparse_t[s, b * 128:(b + 1) * 128, tok] = (values * m).astype(BF16)
            mask_cols[s, tok, b * 128:(b + 1) * 128] = m.T.astype(BF16)


def grad_step(bufs, g, q, sparse_t, grad, base):
    lhs = sparse_t[0:g + 1].reshape((g + 1) * WIDTH, TOKENS)
    out = jnp.dot(lhs, columns(bufs, g, q), preferred_element_type=F32).astype(BF16)
    grad[base:base + g + 1, :, pl.ds(pl.multiple_of(q * 256, 256), 256)] = out.reshape(g + 1, WIDTH, 256)


def feature_step(bufs, g, h, dec, base, total, finish):
    tok = pl.ds(pl.multiple_of(h * 256, 256), 256)
    lhs = rows(bufs, g, h)
    for s in range(g + 1):
        term = lax.dot_general(lhs, dec[base + s], (((1,), (1,)), ((), ())), preferred_element_type=F32)
        if g < LAYERS - 1:
            term = term + total[s, tok]
        if s == g:
            finish(s, tok, term)
        else:
            total[s, tok] = term


def at(table, i):
    for when, events in table:
        @pl.when(i == when)
        def _():
            for event in events:
                event()


def early_kernel(own_ref, act_hbm, mask_hbm, dec_hbm, *rest):
    buf0, (grad, feat, total0, sparse_t, mask_cols, dec0) = rest[:3], rest[3:9]
    later, (act, mask, dec, total, own_sem, send, recv, sem) = rest[9:18], rest[18:]
    bufs = {(g, a): buf0[a] if g == 0 else later[(g - 1) * 3 + a] for g, a in BUFS}
    net = Gather(own_ref, bufs, own_sem, send, recv)
    own = net.own()
    for copy in own:
        copy.start()
    load_act = pltpu.make_async_copy(act_hbm, act, sem.at[0])
    load_mask = pltpu.make_async_copy(mask_hbm, mask, sem.at[5])
    load_act.start()
    load_mask.start()
    net.greet()
    for copy in own:
        copy.wait()
    net.meet()
    for g in TARGETS:
        net.p1(g)
    loads = [pltpu.make_async_copy(dec_hbm.at[pl.ds(6, 4)], dec.at[pl.ds(5, 4)], sem.at[1]),
             pltpu.make_async_copy(dec_hbm.at[pl.ds(3, 3)], dec.at[pl.ds(2, 3)], sem.at[2]),
             pltpu.make_async_copy(dec_hbm.at[pl.ds(1, 2)], dec.at[pl.ds(0, 2)], sem.at[3]),
             pltpu.make_async_copy(dec_hbm.at[pl.ds(0, 1)], dec0, sem.at[4])]
    for load in loads:
        load.start()
    load_act.wait()
    load_mask.wait()
    prepare(0, act, mask, sparse_t, mask_cols)
    prepare(1, act, mask, sparse_t, mask_cols)
    net.p2(3)
    net.p2(2)
    prepare(2, act, mask, sparse_t, mask_cols)
    prepare(3, act, mask, sparse_t, mask_cols)
    net.p3(3)
    net.p2(1)
    net.p2_forward(2)
    net.p3_forward(3)
    net.p2_forward(1)
    net.sides(3)
    net.p3(2)
    net.p2(0)
    net.last(3)
    net.arrived(3)

    def finish(s, tok, term):
        feat[s - 1, tok] = (term * mask_cols[s, tok].astype(F32)).astype(BF16)

    plan = {
        3: ([(1, [lambda: net.p3_forward(2)]), (2, [lambda: net.p2_forward(0), lambda: net.p3(1)]), (5, [lambda: net.sides(2)])],
            [(0, [lambda: net.last(2)]), (3, [lambda: net.p3_forward(1), lambda: net.p3(0)])]),
        2: ([(2, [lambda: net.sides(1)]), (6, [lambda: net.last(1)])],
            [(1, [lambda: net.p3_forward(0)])]),
        1: ([(1, [lambda: net.sides(0)]), (6, [lambda: net.last(0)])], []),
    }
    for i, g in enumerate((3, 2, 1)):
        base = OFFSET[g] - 1
        if g < 3:
            net.arrived(g)
        loads[i].wait()

        @pl.loop(0, 8)
        def _(q):
            at(plan[g][0], q)
            grad_step(bufs, g, q, sparse_t, grad, base)

        @pl.loop(0, 4)
        def _(h):
            at(plan[g][1], h)
            feature_step(bufs, g, h, dec, base, TOTAL(total, total0), finish)
    loads[3].wait()
    net.arrived(0)
    net.finish()


class TOTAL:
    def __init__(self, rest, first):
        self.rest, self.first = rest, first

    def __getitem__(self, key):
        s, tok = key
        return self.first[tok] if s == 0 else self.rest[s - 1, tok]

    def __setitem__(self, key, value):
        s, tok = key
        if s == 0:
            self.first[tok] = value
        else:
            self.rest[s - 1, tok] = value


def late_kernel(*refs):
    buf0, (grad_in, feat_in, total0, sparse_t, mask_cols, dec0), (grad_hbm, feat_hbm, grad, feat, sem) = refs[:3], refs[3:9], refs[9:]
    bufs = {(0, a): buf0[a] for a in range(3)}
    stores = [pltpu.make_async_copy(grad_in, grad_hbm.at[pl.ds(1, PAIRS - 1)], sem.at[0]),
              pltpu.make_async_copy(feat_in, feat_hbm.at[pl.ds(1, LAYERS - 1)], sem.at[1])]
    for out in stores:
        out.start()

    def finish(s, tok, term):
        feat[tok] = (term * mask_cols[0, tok].astype(F32)).astype(BF16)

    @pl.loop(0, 4)
    def _(h):
        feature_step(bufs, 0, h, dec0.at[pl.ds(0, 1)], 0, TOTAL(None, total0), finish)
    stores.append(pltpu.make_async_copy(feat, feat_hbm.at[0], sem.at[2]))
    stores[-1].start()

    @pl.loop(0, 8)
    def _(q):
        grad_step(bufs, 0, q, sparse_t, grad, 0)
    stores.append(pltpu.make_async_copy(grad, grad_hbm.at[pl.ds(0, 1)], sem.at[3]))
    stores[-1].start()
    for out in stores:
        out.wait()


def body(activations, active_blocks, cotangent, decoder):
    vmem, hbm = pl.BlockSpec(memory_space=pltpu.VMEM), pl.BlockSpec(memory_space=pltpu.HBM)
    mask = pltpu.with_memory_space_constraint(jnp.transpose(active_blocks, (0, 2, 1)), pltpu.HBM)
    cotangent = pltpu.with_memory_space_constraint(cotangent, pltpu.HBM)
    sems = len(BUFS) * len(Gather.SLOTS)
    buf = {key: pltpu.VMEM((2, 4, 4, 4, ROWS[key[0]][key[1]], 128), BF16) for key in BUFS}
    passed = pl.pallas_call(
        early_kernel,
        out_shape=[buf[0, a] for a in range(3)] + [
            pltpu.VMEM((PAIRS - 1, WIDTH, D), BF16),
            pltpu.VMEM((LAYERS - 1, TOKENS, WIDTH), BF16),
            pltpu.VMEM((TOKENS, WIDTH), F32),
            pltpu.VMEM((LAYERS, WIDTH, TOKENS), BF16),
            pltpu.VMEM((LAYERS, TOKENS, WIDTH), BF16),
            pltpu.VMEM((1, WIDTH, D), BF16),
        ],
        in_specs=[hbm] * 4,
        out_specs=[vmem] * 9,
        scratch_shapes=[buf[g, a] for g, a in BUFS if g] + [
            pltpu.VMEM((LAYERS, TOKENS, WIDTH), BF16),
            pltpu.VMEM((LAYERS, 2, TOKENS), jnp.int32),
            pltpu.VMEM((PAIRS - 1, WIDTH, D), BF16),
            pltpu.VMEM((LAYERS - 2, TOKENS, WIDTH), F32),
            pltpu.SemaphoreType.DMA((len(BUFS),)),
            pltpu.SemaphoreType.DMA((sems,)),
            pltpu.SemaphoreType.DMA((sems,)),
            pltpu.SemaphoreType.DMA((6,)),
        ],
        compiler_params=pltpu.CompilerParams(collective_id=0, has_side_effects=True, vmem_limit_bytes=EARLY_LIMIT),
        name="gather_and_products",
    )(cotangent, activations, mask, decoder)
    return tuple(pl.pallas_call(
        late_kernel,
        out_shape=[jax.ShapeDtypeStruct((PAIRS, WIDTH, D), BF16), jax.ShapeDtypeStruct((LAYERS, TOKENS, WIDTH), BF16)],
        in_specs=[vmem] * 9,
        out_specs=[hbm, hbm],
        scratch_shapes=[
            pltpu.VMEM((1, WIDTH, D), BF16),
            pltpu.VMEM((TOKENS, WIDTH), BF16),
            pltpu.SemaphoreType.DMA((4,)),
        ],
        compiler_params=pltpu.CompilerParams(vmem_limit_bytes=LATE_LIMIT),
        name="last_products",
    )(*passed))


def solution(mesh):
    in_specs = (
        P(None, None, ("layer", "feat")),
        P(None, None, ("layer", "feat")),
        P(None, "layer", "feat"),
        P(None, ("layer", "feat"), None),
    )
    out_specs = (P(None, ("layer", "feat"), None), P(None, None, ("layer", "feat")))
    return jax.shard_map(body, mesh=mesh, in_specs=in_specs, out_specs=out_specs, check_vma=False)
```

```python
import functools

import jax
import jax.numpy as jnp
from jax import lax
from jax.experimental import pallas as pl
from jax.experimental.pallas import tpu as pltpu
from jax.sharding import PartitionSpec as P

MESH = pl.DeviceIdType.MESH
LAYERS, TOKENS, D, WIDTH = 4, 1024, 2048, 256
PAIRS = LAYERS * (LAYERS + 1) // 2
ROWS = {3: (48, 48, 32), 2: (48, 32, 48), 1: (32, 48, 48), 0: (48, 48, 32)}
START = {g: (0, r[0], r[0] + r[1]) for g, r in ROWS.items()}
ORDER = ((0, 1, 2), (1, 2, 0), (2, 0, 1))
TARGETS = (3, 2, 1, 0)
OFFSET = (0, 1, 3, 6)
BUFS = [(g, a) for g in range(LAYERS) for a in range(3)]
BF16, F32 = jnp.bfloat16, jnp.float32
DIRECT = (3, 2)
PIECES = (2, 2, 2, 2)
STEPS = (2, 2, 2, 4)
SCHEDULE = (
    "p1 3", "p1 2", "p1 0", "p1 1", "prep 0", "prep 1", "prep 2", "prep 3", "p2 3", "p2 0", "p2 2", "p2 1",
    "p3 3", "p2f 1", "p2f 0", "p3f 3", "p3 2", "sides 3", "p3 1", "last 3", "p3f 2", "p3 0", "work 3 0",
    "sides 2", "work 3 1", "work 3 2", "last 2", "p3f 1", "work 3 3", "p3f 0", "sides 1", "work 2 0", "last 1",
    "sides 0", "work 2 1", "last 0", "work 1 0", "work 1 1",
)
EARLY_LIMIT, LATE_LIMIT = 36 * 2**20, 6 * 2**20


def position():
    layer, feat = lax.axis_index("layer"), lax.axis_index("feat")
    x, zh = lax.rem(layer, 4), layer // 4
    core, y, zl = lax.rem(feat, 2), lax.rem(feat // 2, 4), feat // 8
    return (x, y, zh * 2 + zl), core


def device_id(c, core):
    x, y, z = c
    return ((z // 2) * 4 + x, (lax.rem(z, 2) * 4 + y) * 2 + core)


def shifted(c, axis, by):
    return tuple(lax.rem(v + by + 4, 4) if i == axis else v for i, v in enumerate(c))


SLOTS = {g: ("1L", "1R", "1O", "2L", "2R", "2O", *(f"3{side}{i}" for side in "LRO" for i in range(PIECES[g])), "p0", "pL", "pR", "pO")
         for g in range(LAYERS)}
INDEX = {key: i for i, key in enumerate((g, a, slot) for g in SLOTS for a in range(3) for slot in SLOTS[g])}


class Gather:
    def __init__(self, own_ref, bufs, own_sem, send, recv):
        self.c, self.core = position()
        self.own_ref, self.bufs = own_ref, bufs
        self.own_sem, self.send, self.recv = own_sem, send, recv

    def near(self, axis, by):
        return device_id(shifted(self.c, axis, by), self.core)

    def greet(self):
        sem = pltpu.get_barrier_semaphore()
        for peer in self.peers():
            pl.semaphore_signal(sem, inc=1, device_id=peer, device_id_type=MESH)

    def peers(self):
        out = [self.near(axis, by) for axis in range(3) for by in (1, -1, 2)]
        return out + [device_id(self.c, 1 - self.core)]

    def meet(self):
        pl.semaphore_wait(pltpu.get_barrier_semaphore(), 10)

    def own(self):
        out = []
        for i, (g, a) in enumerate(BUFS):
            c1, c2, c3 = (self.c[k] for k in ORDER[a])
            out.append(pltpu.make_async_copy(
                self.own_ref.at[g, pl.ds(START[g][a], ROWS[g][a])],
                self.bufs[g, a].at[self.core, c3, c2, c1], self.own_sem.at[i]))
        return out

    def copy(self, g, a, slot):
        phase, side = slot[0], slot[1]
        axis = ORDER[a][2 if phase == "p" else int(phase) - 1]
        by = 0
        if phase == "p":
            by = {"0": 0, "L": -1, "R": 1, "O": 2}[side]
            to = device_id(self.c, 1 - self.core)
        elif side == "O":
            if phase == "1" or (phase == "2" and g in DIRECT):
                to = self.near(axis, 2)
            else:
                by = (-1 if int(slot[2]) < PIECES[g] // 2 else 1) if phase == "3" else (-1 if (g + a) % 2 else 1)
                to = self.near(axis, -by)
        else:
            to = self.near(axis, 1 if side == "L" else -1)
        c1, c2, c3 = (shifted(self.c, axis, by)[k] for k in ORDER[a])
        buf = self.bufs[g, a].at[self.core, c3]
        if phase == "1":
            buf = buf.at[c2, c1]
        elif phase == "2":
            buf = buf.at[c2]
        elif phase == "3":
            size = 4 // PIECES[g]
            buf = buf.at[pl.ds(size * int(slot[2]), size)]
        i = INDEX[g, a, slot]
        return pltpu.make_async_remote_copy(
            src_ref=buf, dst_ref=buf, send_sem=self.send.at[i], recv_sem=self.recv.at[i],
            device_id=to, device_id_type=MESH)

    def go(self, g, a, *slots):
        for slot in slots:
            self.copy(g, a, slot).start()

    def wait(self, g, a, *slots):
        for slot in slots:
            self.copy(g, a, slot).wait_recv()

    def p1(self, g):
        for a in range(3):
            self.go(g, a, "1O", "1L", "1R")

    def p2(self, g):
        for a in range(3):
            self.wait(g, a, "1O", "1L", "1R")
            if g in DIRECT:
                self.go(g, a, "2O")
            self.go(g, a, "2L", "2R")

    def p2f(self, g):
        for a in range(3):
            self.wait(g, a, "2L", "2R")
            self.go(g, a, "2O")

    def p3(self, g):
        for a in range(3):
            if g in DIRECT:
                self.wait(g, a, "2L", "2R")
            self.wait(g, a, "2O")
            for i in range(PIECES[g]):
                self.go(g, a, f"3L{i}", f"3R{PIECES[g] - 1 - i}")
        for a in range(3):
            self.go(g, a, "p0")

    def p3_forward(self, g, i):
        for a in range(3):
            self.wait(g, a, f"3L{i}")
            self.go(g, a, f"3O{i}")
            j = PIECES[g] - 1 - i
            self.wait(g, a, f"3R{j}")
            self.go(g, a, f"3O{j}")

    def p3f(self, g):
        self.p3_forward(g, 0)

    def p3g(self, g):
        self.p3_forward(g, 1)

    def sides(self, g):
        half = PIECES[g] // 2
        for a in range(3):
            for i in range(half):
                self.wait(g, a, f"3L{half + i}")
            self.go(g, a, "pL")
            for i in range(half):
                self.wait(g, a, f"3R{i}")
            self.go(g, a, "pR")

    def last(self, g):
        for a in range(3):
            for i in range(PIECES[g]):
                self.wait(g, a, f"3O{i}")
            self.go(g, a, "pO")

    def arrived(self, g):
        for a in range(3):
            self.wait(g, a, "p0", "pL", "pR", "pO")

    def finish(self):
        for g, a in BUFS:
            for slot in SLOTS[g]:
                self.copy(g, a, slot).wait_send()


def block(bufs, g, x, y, z, core):
    parts = []
    for a in range(3):
        c1, c2, c3 = ((x, y, z)[k] for k in ORDER[a])
        parts.append(bufs[g, a][core, c3, c2, c1])
    return jnp.concatenate(parts, axis=0)


def columns(bufs, g, q):
    zl, y = q // 4, lax.rem(q, 4)
    return jnp.concatenate(
        [jnp.concatenate([block(bufs, g, l % 4, y, (l // 4) * 2 + zl, core) for l in range(8)], axis=0)
         for core in range(2)], axis=1)


def rows(bufs, g, h):
    zh = h // 2
    out = []
    for i in range(2):
        x = lax.rem(h, 2) * 2 + i
        out.append(jnp.concatenate(
            [block(bufs, g, x, (f // 2) % 4, zh * 2 + f // 8, f % 2) for f in range(16)], axis=1))
    return jnp.concatenate(out, axis=0)


def prepare(s, act, mask, sparse_t, mask_cols):
    @pl.loop(0, 8)
    def _(l):
        tok = pl.ds(pl.multiple_of(l * 128, 128), 128)
        for b in range(2):
            m = jnp.broadcast_to(mask[s, b:b + 1, tok].astype(F32), (128, 128))
            values = act[s, tok, b * 128:(b + 1) * 128].astype(F32).T
            sparse_t[s, b * 128:(b + 1) * 128, tok] = (values * m).astype(BF16)
            mask_cols[s, tok, b * 128:(b + 1) * 128] = m.T.astype(BF16)


def work(bufs, g, i, sparse_t, grad, dec, base, total, finish):
    size, count = D // STEPS[g], TOKENS // STEPS[g]
    lhs = sparse_t[0:g + 1].reshape((g + 1) * WIDTH, TOKENS)
    blocks = size // 256
    rhs = jnp.concatenate([columns(bufs, g, i * blocks + k) for k in range(blocks)], axis=1)
    out = jnp.dot(lhs, rhs, preferred_element_type=F32).astype(BF16)
    grad[base:base + g + 1, :, pl.ds(pl.multiple_of(i * size, size), size)] = out.reshape(g + 1, WIDTH, size)
    tok = pl.ds(pl.multiple_of(i * count, count), count)
    blocks = count // 256
    lhs = jnp.concatenate([rows(bufs, g, i * blocks + k) for k in range(blocks)], axis=0)
    rhs = dec[base:base + g + 1].reshape((g + 1) * WIDTH, D)
    terms = lax.dot_general(lhs, rhs, (((1,), (1,)), ((), ())), preferred_element_type=F32)
    for s in range(g + 1):
        term = terms[:, s * WIDTH:(s + 1) * WIDTH]
        if g < LAYERS - 1:
            term = term + total[s, tok]
        if s == g:
            finish(s, tok, term)
        else:
            total[s, tok] = term


def plan():
    before, steps = {}, []
    for entry in SCHEDULE:
        name, *numbers = entry.split()
        numbers = [int(v) for v in numbers]
        if name in ("prep", "work"):
            before[name, *numbers] = steps
            steps = []
        else:
            steps.append((name, numbers[0]))
    return before, steps


def run(net, steps):
    for name, g in steps:
        getattr(net, name)(g)


def at(net, before, g, i):
    for k in range(1, STEPS[g]):
        if before["work", g, k]:
            @pl.when(i == k)
            def _():
                run(net, before["work", g, k])


def early_kernel(own_ref, act_hbm, mask_hbm, dec_hbm, *rest):
    buf0, (grad, feat, total0, sparse_t, mask_cols, dec0) = rest[:3], rest[3:9]
    later, (act, mask, dec, total, own_sem, send, recv, sem) = rest[9:18], rest[18:]
    bufs = {(g, a): buf0[a] if g == 0 else later[(g - 1) * 3 + a] for g, a in BUFS}
    net = Gather(own_ref, bufs, own_sem, send, recv)
    own = net.own()
    for copy in own:
        copy.start()
    load_act = pltpu.make_async_copy(act_hbm, act, sem.at[0])
    load_mask = pltpu.make_async_copy(mask_hbm, mask, sem.at[5])
    load_act.start()
    load_mask.start()
    net.greet()
    for copy in own:
        copy.wait()
    net.meet()
    loads = [pltpu.make_async_copy(dec_hbm.at[pl.ds(6, 4)], dec.at[pl.ds(5, 4)], sem.at[1]),
             pltpu.make_async_copy(dec_hbm.at[pl.ds(3, 3)], dec.at[pl.ds(2, 3)], sem.at[2]),
             pltpu.make_async_copy(dec_hbm.at[pl.ds(1, 2)], dec.at[pl.ds(0, 2)], sem.at[3]),
             pltpu.make_async_copy(dec_hbm.at[pl.ds(0, 1)], dec0, sem.at[4])]

    def finish(s, tok, term):
        feat[s - 1, tok] = (term * mask_cols[s, tok].astype(F32)).astype(BF16)

    before, tail = plan()
    for s in range(LAYERS):
        run(net, before["prep", s])
        if s == 0:
            for load in loads:
                load.start()
            load_act.wait()
            load_mask.wait()
        prepare(s, act, mask, sparse_t, mask_cols)
    for i, g in enumerate((3, 2, 1)):
        base = OFFSET[g] - 1
        run(net, before["work", g, 0])
        net.arrived(g)
        loads[i].wait()

        @pl.loop(0, STEPS[g])
        def _(k):
            at(net, before, g, k)
            work(bufs, g, k, sparse_t, grad, dec, base, TOTAL(total, total0), finish)
    run(net, tail)
    loads[3].wait()
    net.arrived(0)
    net.finish()


class TOTAL:
    def __init__(self, rest, first):
        self.rest, self.first = rest, first

    def __getitem__(self, key):
        s, tok = key
        return self.first[tok] if s == 0 else self.rest[s - 1, tok]

    def __setitem__(self, key, value):
        s, tok = key
        if s == 0:
            self.first[tok] = value
        else:
            self.rest[s - 1, tok] = value


def late_kernel(*refs):
    buf0, (grad_in, feat_in, total0, sparse_t, mask_cols, dec0), (grad_hbm, feat_hbm, grad, feat, sem) = refs[:3], refs[3:9], refs[9:]
    bufs = {(0, a): buf0[a] for a in range(3)}
    stores = [pltpu.make_async_copy(grad_in, grad_hbm.at[pl.ds(1, PAIRS - 1)], sem.at[0]),
              pltpu.make_async_copy(feat_in, feat_hbm.at[pl.ds(1, LAYERS - 1)], sem.at[1])]
    for out in stores:
        out.start()

    def finish(s, tok, term):
        feat[tok] = (term * mask_cols[0, tok].astype(F32)).astype(BF16)

    @pl.loop(0, STEPS[0])
    def _(k):
        work(bufs, 0, k, sparse_t, grad, dec0, 0, TOTAL(None, total0), finish)
    stores += [pltpu.make_async_copy(feat, feat_hbm.at[0], sem.at[2]),
               pltpu.make_async_copy(grad, grad_hbm.at[pl.ds(0, 1)], sem.at[3])]
    for out in stores[2:]:
        out.start()
    for out in stores:
        out.wait()


def body(activations, active_blocks, cotangent, decoder):
    vmem, hbm = pl.BlockSpec(memory_space=pltpu.VMEM), pl.BlockSpec(memory_space=pltpu.HBM)
    mask = pltpu.with_memory_space_constraint(jnp.transpose(active_blocks, (0, 2, 1)), pltpu.HBM)
    cotangent = pltpu.with_memory_space_constraint(cotangent, pltpu.HBM)
    sems = len(INDEX)
    buf = {key: pltpu.VMEM((2, 4, 4, 4, ROWS[key[0]][key[1]], 128), BF16) for key in BUFS}
    passed = pl.pallas_call(
        early_kernel,
        out_shape=[buf[0, a] for a in range(3)] + [
            pltpu.VMEM((PAIRS - 1, WIDTH, D), BF16),
            pltpu.VMEM((LAYERS - 1, TOKENS, WIDTH), BF16),
            pltpu.VMEM((TOKENS, WIDTH), F32),
            pltpu.VMEM((LAYERS, WIDTH, TOKENS), BF16),
            pltpu.VMEM((LAYERS, TOKENS, WIDTH), BF16),
            pltpu.VMEM((1, WIDTH, D), BF16),
        ],
        in_specs=[hbm] * 4,
        out_specs=[vmem] * 9,
        scratch_shapes=[buf[g, a] for g, a in BUFS if g] + [
            pltpu.VMEM((LAYERS, TOKENS, WIDTH), BF16),
            pltpu.VMEM((LAYERS, 2, TOKENS), jnp.int32),
            pltpu.VMEM((PAIRS - 1, WIDTH, D), BF16),
            pltpu.VMEM((LAYERS - 2, TOKENS, WIDTH), F32),
            pltpu.SemaphoreType.DMA((len(BUFS),)),
            pltpu.SemaphoreType.DMA((sems,)),
            pltpu.SemaphoreType.DMA((sems,)),
            pltpu.SemaphoreType.DMA((6,)),
        ],
        compiler_params=pltpu.CompilerParams(collective_id=0, has_side_effects=True, vmem_limit_bytes=EARLY_LIMIT),
        name="gather_and_products",
    )(cotangent, activations, mask, decoder)
    return tuple(pl.pallas_call(
        late_kernel,
        out_shape=[jax.ShapeDtypeStruct((PAIRS, WIDTH, D), BF16), jax.ShapeDtypeStruct((LAYERS, TOKENS, WIDTH), BF16)],
        in_specs=[vmem] * 9,
        out_specs=[hbm, hbm],
        scratch_shapes=[
            pltpu.VMEM((1, WIDTH, D), BF16),
            pltpu.VMEM((TOKENS, WIDTH), BF16),
            pltpu.SemaphoreType.DMA((4,)),
        ],
        compiler_params=pltpu.CompilerParams(vmem_limit_bytes=LATE_LIMIT),
        name="last_products",
    )(*passed))


def solution(mesh):
    in_specs = (
        P(None, None, ("layer", "feat")),
        P(None, None, ("layer", "feat")),
        P(None, "layer", "feat"),
        P(None, ("layer", "feat"), None),
    )
    out_specs = (P(None, ("layer", "feat"), None), P(None, None, ("layer", "feat")))
    return jax.shard_map(body, mesh=mesh, in_specs=in_specs, out_specs=out_specs, check_vma=False)
```

```python
import functools

import jax
import jax.numpy as jnp
from jax import lax
from jax.experimental import pallas as pl
from jax.experimental.pallas import tpu as pltpu
from jax.sharding import PartitionSpec as P

MESH = pl.DeviceIdType.MESH
LAYERS, TOKENS, D, WIDTH = 4, 1024, 2048, 256
PAIRS = LAYERS * (LAYERS + 1) // 2
ROWS = {3: (48, 48, 32), 2: (48, 32, 48), 1: (32, 48, 48), 0: (48, 48, 32)}
START = {g: (0, r[0], r[0] + r[1]) for g, r in ROWS.items()}
ORDER = ((0, 1, 2), (1, 2, 0), (2, 0, 1))
TARGETS = (3, 2, 1, 0)
OFFSET = (0, 1, 3, 6)
BUFS = [(g, a) for g in range(LAYERS) for a in range(3)]
BF16, F32 = jnp.bfloat16, jnp.float32
DIRECT = (3, 2)
PIECES = (2, 2, 2, 2)
STEPS = (2, 2, 2, 4)
SPLIT, OWN_STEPS = (3,), 1
SCHEDULE = (
    "p1 3", "p1 2", "p1 0", "p1 1", "prep 0", "prep 1", "prep 2", "prep 3", "p2 3", "p2 0", "p2 2", "p2 1",
    "p3 3", "p2f 1", "p2f 0", "p3f 3", "p3 2", "p3 1", "sides 3", "last 3", "own 3 0", "p3f 2", "p3 0",
    "work 3 0", "sides 2", "work 3 1", "work 3 2", "last 2", "p3f 1", "work 3 3", "p3f 0", "sides 1", "work 2 0",
    "last 1", "sides 0", "work 2 1", "last 0", "work 1 0", "work 1 1",
)
EARLY_LIMIT, LATE_LIMIT = 36 * 2**20, 6 * 2**20


def position():
    layer, feat = lax.axis_index("layer"), lax.axis_index("feat")
    x, zh = lax.rem(layer, 4), layer // 4
    core, y, zl = lax.rem(feat, 2), lax.rem(feat // 2, 4), feat // 8
    return (x, y, zh * 2 + zl), core


def device_id(c, core):
    x, y, z = c
    return ((z // 2) * 4 + x, (lax.rem(z, 2) * 4 + y) * 2 + core)


def shifted(c, axis, by):
    return tuple(lax.rem(v + by + 4, 4) if i == axis else v for i, v in enumerate(c))


SLOTS = {g: ("1L", "1R", "1O", "2L", "2R", "2O", *(f"3{side}{i}" for side in "LRO" for i in range(PIECES[g])), "p0", "pL", "pR", "pO")
         for g in range(LAYERS)}
INDEX = {key: i for i, key in enumerate((g, a, slot) for g in SLOTS for a in range(3) for slot in SLOTS[g])}


class Gather:
    def __init__(self, own_ref, bufs, own_sem, send, recv):
        self.c, self.core = position()
        self.own_ref, self.bufs = own_ref, bufs
        self.own_sem, self.send, self.recv = own_sem, send, recv

    def near(self, axis, by):
        return device_id(shifted(self.c, axis, by), self.core)

    def greet(self):
        sem = pltpu.get_barrier_semaphore()
        for peer in self.peers():
            pl.semaphore_signal(sem, inc=1, device_id=peer, device_id_type=MESH)

    def peers(self):
        out = [self.near(axis, by) for axis in range(3) for by in (1, -1, 2)]
        return out + [device_id(self.c, 1 - self.core)]

    def meet(self):
        pl.semaphore_wait(pltpu.get_barrier_semaphore(), 10)

    def own(self):
        out = []
        for i, (g, a) in enumerate(BUFS):
            c1, c2, c3 = (self.c[k] for k in ORDER[a])
            out.append(pltpu.make_async_copy(
                self.own_ref.at[g, pl.ds(START[g][a], ROWS[g][a])],
                self.bufs[g, a].at[self.core, c3, c2, c1], self.own_sem.at[i]))
        return out

    def copy(self, g, a, slot):
        phase, side = slot[0], slot[1]
        axis = ORDER[a][2 if phase == "p" else int(phase) - 1]
        by = 0
        if phase == "p":
            by = {"0": 0, "L": -1, "R": 1, "O": 2}[side]
            to = device_id(self.c, 1 - self.core)
        elif side == "O":
            if phase == "1" or (phase == "2" and g in DIRECT):
                to = self.near(axis, 2)
            else:
                by = (-1 if int(slot[2]) < PIECES[g] // 2 else 1) if phase == "3" else (-1 if (g + a) % 2 else 1)
                to = self.near(axis, -by)
        else:
            to = self.near(axis, 1 if side == "L" else -1)
        c1, c2, c3 = (shifted(self.c, axis, by)[k] for k in ORDER[a])
        buf = self.bufs[g, a].at[self.core, c3]
        if phase == "1":
            buf = buf.at[c2, c1]
        elif phase == "2":
            buf = buf.at[c2]
        elif phase == "3":
            size = 4 // PIECES[g]
            buf = buf.at[pl.ds(size * int(slot[2]), size)]
        i = INDEX[g, a, slot]
        return pltpu.make_async_remote_copy(
            src_ref=buf, dst_ref=buf, send_sem=self.send.at[i], recv_sem=self.recv.at[i],
            device_id=to, device_id_type=MESH)

    def go(self, g, a, *slots):
        for slot in slots:
            self.copy(g, a, slot).start()

    def wait(self, g, a, *slots):
        for slot in slots:
            self.copy(g, a, slot).wait_recv()

    def p1(self, g):
        for a in range(3):
            self.go(g, a, "1O", "1L", "1R")

    def p2(self, g):
        for a in range(3):
            self.wait(g, a, "1O", "1L", "1R")
            if g in DIRECT:
                self.go(g, a, "2O")
            self.go(g, a, "2L", "2R")

    def p2f(self, g):
        for a in range(3):
            self.wait(g, a, "2L", "2R")
            self.go(g, a, "2O")

    def p3(self, g):
        for a in range(3):
            if g in DIRECT:
                self.wait(g, a, "2L", "2R")
            self.wait(g, a, "2O")
            for i in range(PIECES[g]):
                self.go(g, a, f"3L{i}", f"3R{PIECES[g] - 1 - i}")
        for a in range(3):
            self.go(g, a, "p0")

    def p3_forward(self, g, i):
        for a in range(3):
            self.wait(g, a, f"3L{i}")
            self.go(g, a, f"3O{i}")
            j = PIECES[g] - 1 - i
            self.wait(g, a, f"3R{j}")
            self.go(g, a, f"3O{j}")

    def p3f(self, g):
        self.p3_forward(g, 0)

    def p3g(self, g):
        self.p3_forward(g, 1)

    def sides(self, g):
        half = PIECES[g] // 2
        for a in range(3):
            for i in range(half):
                self.wait(g, a, f"3L{half + i}")
            self.go(g, a, "pL")
            for i in range(half):
                self.wait(g, a, f"3R{i}")
            self.go(g, a, "pR")

    def last(self, g):
        for a in range(3):
            for i in range(PIECES[g]):
                self.wait(g, a, f"3O{i}")
            self.go(g, a, "pO")

    def arrived(self, g):
        for a in range(3):
            self.wait(g, a, "p0", "pL", "pR", "pO")

    def finish(self):
        for g, a in BUFS:
            for slot in SLOTS[g]:
                self.copy(g, a, slot).wait_send()


def block(bufs, g, x, y, z, core):
    parts = []
    for a in range(3):
        c1, c2, c3 = ((x, y, z)[k] for k in ORDER[a])
        parts.append(bufs[g, a][core, c3, c2, c1])
    return jnp.concatenate(parts, axis=0)


def columns(bufs, g, q):
    zl, y = q // 4, lax.rem(q, 4)
    return jnp.concatenate(
        [jnp.concatenate([block(bufs, g, l % 4, y, (l // 4) * 2 + zl, core) for l in range(8)], axis=0)
         for core in range(2)], axis=1)


def rows(bufs, g, h):
    zh = h // 2
    out = []
    for i in range(2):
        x = lax.rem(h, 2) * 2 + i
        out.append(jnp.concatenate(
            [block(bufs, g, x, (f // 2) % 4, zh * 2 + f // 8, f % 2) for f in range(16)], axis=1))
    return jnp.concatenate(out, axis=0)


def prepare(s, act, mask, sparse_t, mask_cols):
    @pl.loop(0, 8)
    def _(l):
        tok = pl.ds(pl.multiple_of(l * 128, 128), 128)
        for b in range(2):
            m = jnp.broadcast_to(mask[s, b:b + 1, tok].astype(F32), (128, 128))
            values = act[s, tok, b * 128:(b + 1) * 128].astype(F32).T
            sparse_t[s, b * 128:(b + 1) * 128, tok] = (values * m).astype(BF16)
            mask_cols[s, tok, b * 128:(b + 1) * 128] = m.T.astype(BF16)


def panel_products(bufs, g, panels, sparse_t, grad, base):
    lhs = sparse_t[0:g + 1].reshape((g + 1) * WIDTH, TOKENS)
    rhs = jnp.concatenate(
        [jnp.concatenate([block(bufs, g, l % 4, y, (l // 4) * 2 + zl, core) for l in range(8)], axis=0)
         for zl, y, core in panels], axis=1)
    out = jnp.dot(lhs, rhs, preferred_element_type=F32).astype(BF16)
    for k, (zl, y, core) in enumerate(panels):
        at = pl.ds(pl.multiple_of(((zl * 4 + y) * 2 + core) * 128, 128), 128)
        grad[base:base + g + 1, :, at] = out[:, k * 128:(k + 1) * 128].reshape(g + 1, WIDTH, 128)


def own_work(bufs, g, i, sparse_t, grad, base):
    core = position()[1]
    panels = [(i, y, core) for y in range(4)] if OWN_STEPS == 2 else [(zl, y, core) for zl in range(2) for y in range(4)]
    panel_products(bufs, g, panels, sparse_t, grad, base)


def work(bufs, g, i, sparse_t, grad, dec, base, total, finish):
    size, count = D // STEPS[g], TOKENS // STEPS[g]
    blocks = size // 256
    if g in SPLIT:
        other = 1 - position()[1]
        panels = [((i * blocks + k) // 4, lax.rem(i * blocks + k, 4), other) for k in range(blocks)]
        panel_products(bufs, g, panels, sparse_t, grad, base)
    else:
        lhs = sparse_t[0:g + 1].reshape((g + 1) * WIDTH, TOKENS)
        rhs = jnp.concatenate([columns(bufs, g, i * blocks + k) for k in range(blocks)], axis=1)
        out = jnp.dot(lhs, rhs, preferred_element_type=F32).astype(BF16)
        grad[base:base + g + 1, :, pl.ds(pl.multiple_of(i * size, size), size)] = out.reshape(g + 1, WIDTH, size)
    tok = pl.ds(pl.multiple_of(i * count, count), count)
    blocks = count // 256
    lhs = jnp.concatenate([rows(bufs, g, i * blocks + k) for k in range(blocks)], axis=0)
    rhs = dec[base:base + g + 1].reshape((g + 1) * WIDTH, D)
    terms = lax.dot_general(lhs, rhs, (((1,), (1,)), ((), ())), preferred_element_type=F32)
    for s in range(g + 1):
        term = terms[:, s * WIDTH:(s + 1) * WIDTH]
        if g < LAYERS - 1:
            term = term + total[s, tok]
        if s == g:
            finish(s, tok, term)
        else:
            total[s, tok] = term


def plan():
    before, steps = {}, []
    for entry in SCHEDULE:
        name, *numbers = entry.split()
        numbers = [int(v) for v in numbers]
        if name in ("prep", "work", "own"):
            before[name, *numbers] = steps
            steps = []
        else:
            steps.append((name, numbers[0]))
    return before, steps


def run(net, steps):
    for name, g in steps:
        getattr(net, name)(g)


def at(net, before, g, i):
    for k in range(1, STEPS[g]):
        if before["work", g, k]:
            @pl.when(i == k)
            def _():
                run(net, before["work", g, k])


def early_kernel(own_ref, act_hbm, mask_hbm, dec_hbm, *rest):
    buf0, (grad, feat, total0, sparse_t, mask_cols, dec0) = rest[:3], rest[3:9]
    later, (act, mask, dec, total, own_sem, send, recv, sem) = rest[9:18], rest[18:]
    bufs = {(g, a): buf0[a] if g == 0 else later[(g - 1) * 3 + a] for g, a in BUFS}
    net = Gather(own_ref, bufs, own_sem, send, recv)
    own = net.own()
    for copy in own:
        copy.start()
    load_act = pltpu.make_async_copy(act_hbm, act, sem.at[0])
    load_mask = pltpu.make_async_copy(mask_hbm, mask, sem.at[5])
    load_act.start()
    load_mask.start()
    net.greet()
    for copy in own:
        copy.wait()
    net.meet()
    loads = [pltpu.make_async_copy(dec_hbm.at[pl.ds(6, 4)], dec.at[pl.ds(5, 4)], sem.at[1]),
             pltpu.make_async_copy(dec_hbm.at[pl.ds(3, 3)], dec.at[pl.ds(2, 3)], sem.at[2]),
             pltpu.make_async_copy(dec_hbm.at[pl.ds(1, 2)], dec.at[pl.ds(0, 2)], sem.at[3]),
             pltpu.make_async_copy(dec_hbm.at[pl.ds(0, 1)], dec0, sem.at[4])]

    def finish(s, tok, term):
        feat[s - 1, tok] = term.astype(BF16) * mask_cols[s, tok]

    before, tail = plan()
    for s in range(LAYERS):
        run(net, before["prep", s])
        if s == 0:
            for load in loads:
                load.start()
            load_act.wait()
            load_mask.wait()
        prepare(s, act, mask, sparse_t, mask_cols)
    for i, g in enumerate((3, 2, 1)):
        base = OFFSET[g] - 1
        if g in SPLIT:
            run(net, before["own", g, 0])

            @pl.loop(0, OWN_STEPS)
            def _(k):
                if OWN_STEPS > 1 and before["own", g, 1]:
                    pl.when(k == 1)(lambda: run(net, before["own", g, 1]))
                own_work(bufs, g, k, sparse_t, grad, base)
        run(net, before["work", g, 0])
        net.arrived(g)
        loads[i].wait()

        @pl.loop(0, STEPS[g])
        def _(k):
            at(net, before, g, k)
            work(bufs, g, k, sparse_t, grad, dec, base, TOTAL(total, total0), finish)
    run(net, tail)
    loads[3].wait()
    net.arrived(0)
    net.finish()


class TOTAL:
    def __init__(self, rest, first):
        self.rest, self.first = rest, first

    def __getitem__(self, key):
        s, tok = key
        return self.first[tok] if s == 0 else self.rest[s - 1, tok]

    def __setitem__(self, key, value):
        s, tok = key
        if s == 0:
            self.first[tok] = value
        else:
            self.rest[s - 1, tok] = value


def late_kernel(*refs):
    buf0, (grad_in, feat_in, total0, sparse_t, mask_cols, dec0), (grad_hbm, feat_hbm, grad, feat, sem) = refs[:3], refs[3:9], refs[9:]
    bufs = {(0, a): buf0[a] for a in range(3)}
    stores = [pltpu.make_async_copy(grad_in, grad_hbm.at[pl.ds(1, PAIRS - 1)], sem.at[0]),
              pltpu.make_async_copy(feat_in, feat_hbm.at[pl.ds(1, LAYERS - 1)], sem.at[1])]
    for out in stores:
        out.start()

    def finish(s, tok, term):
        feat[tok] = term.astype(BF16) * mask_cols[0, tok]

    @pl.loop(0, STEPS[0])
    def _(k):
        work(bufs, 0, k, sparse_t, grad, dec0, 0, TOTAL(None, total0), finish)
    stores += [pltpu.make_async_copy(feat, feat_hbm.at[0], sem.at[2]),
               pltpu.make_async_copy(grad, grad_hbm.at[pl.ds(0, 1)], sem.at[3])]
    for out in stores[2:]:
        out.start()
    for out in stores:
        out.wait()


def body(activations, active_blocks, cotangent, decoder):
    vmem, hbm = pl.BlockSpec(memory_space=pltpu.VMEM), pl.BlockSpec(memory_space=pltpu.HBM)
    mask = pltpu.with_memory_space_constraint(jnp.transpose(active_blocks, (0, 2, 1)), pltpu.HBM)
    cotangent = pltpu.with_memory_space_constraint(cotangent, pltpu.HBM)
    sems = len(INDEX)
    buf = {key: pltpu.VMEM((2, 4, 4, 4, ROWS[key[0]][key[1]], 128), BF16) for key in BUFS}
    passed = pl.pallas_call(
        early_kernel,
        out_shape=[buf[0, a] for a in range(3)] + [
            pltpu.VMEM((PAIRS - 1, WIDTH, D), BF16),
            pltpu.VMEM((LAYERS - 1, TOKENS, WIDTH), BF16),
            pltpu.VMEM((TOKENS, WIDTH), F32),
            pltpu.VMEM((LAYERS, WIDTH, TOKENS), BF16),
            pltpu.VMEM((LAYERS, TOKENS, WIDTH), BF16),
            pltpu.VMEM((1, WIDTH, D), BF16),
        ],
        in_specs=[hbm] * 4,
        out_specs=[vmem] * 9,
        scratch_shapes=[buf[g, a] for g, a in BUFS if g] + [
            pltpu.VMEM((LAYERS, TOKENS, WIDTH), BF16),
            pltpu.VMEM((LAYERS, 2, TOKENS), jnp.int32),
            pltpu.VMEM((PAIRS - 1, WIDTH, D), BF16),
            pltpu.VMEM((LAYERS - 2, TOKENS, WIDTH), F32),
            pltpu.SemaphoreType.DMA((len(BUFS),)),
            pltpu.SemaphoreType.DMA((sems,)),
            pltpu.SemaphoreType.DMA((sems,)),
            pltpu.SemaphoreType.DMA((6,)),
        ],
        compiler_params=pltpu.CompilerParams(collective_id=0, has_side_effects=True, vmem_limit_bytes=EARLY_LIMIT),
        name="gather_and_products",
    )(cotangent, activations, mask, decoder)
    return tuple(pl.pallas_call(
        late_kernel,
        out_shape=[jax.ShapeDtypeStruct((PAIRS, WIDTH, D), BF16), jax.ShapeDtypeStruct((LAYERS, TOKENS, WIDTH), BF16)],
        in_specs=[vmem] * 9,
        out_specs=[hbm, hbm],
        scratch_shapes=[
            pltpu.VMEM((1, WIDTH, D), BF16),
            pltpu.VMEM((TOKENS, WIDTH), BF16),
            pltpu.SemaphoreType.DMA((4,)),
        ],
        compiler_params=pltpu.CompilerParams(vmem_limit_bytes=LATE_LIMIT),
        name="last_products",
    )(*passed))


def solution(mesh):
    in_specs = (
        P(None, None, ("layer", "feat")),
        P(None, None, ("layer", "feat")),
        P(None, "layer", "feat"),
        P(None, ("layer", "feat"), None),
    )
    out_specs = (P(None, ("layer", "feat"), None), P(None, None, ("layer", "feat")))
    return jax.shard_map(body, mesh=mesh, in_specs=in_specs, out_specs=out_specs, check_vma=False)
```
